32 devices in a mesh: dp: 16 (over z, x, core), ctx: 2 (over y).
Axes of the slice: x: 2, y: 2, z: 4, core: 2. Of those that a mesh axis runs over, the one named last changes fastest.
Arguments:
- queries: bfloat16 [16, 512, 2048], P('dp', 'ctx'), may hold values from -48 to 48
- key_store: bfloat16 [16, 512, 2048], P('dp', 'ctx'), may hold values from -4 to 4
- value_store: bfloat16 [16, 512, 2048], P('dp', 'ctx'), may hold values from -5 to 5
- kv_exponents: int32 [16, 4, 16], P('dp', 'ctx'), may hold values from -1 to 1
- valid_length: int32 [16], P('dp'), may hold values from 64 to 512, as said below
- round_index: int32 [1], replicated, may hold values from 0 to 63
- out_grad: bfloat16 [16, 512, 2048], P('dp', None, 'ctx'), may hold values from -6 to 6
- params: bfloat16 [16, 2048, 2048], P('dp', None, 'ctx'), may hold values from -6 to 6
- tracker: bfloat16 [16, 2048, 2048], P('dp', None, 'ctx'), may hold values from -6 to 6
- old_grad: bfloat16 [16, 2048, 2048], P('dp', None, 'ctx'), may hold values from -6 to 6
Outputs:
- new_params: bfloat16 [16, 2048, 2048], P('dp', None, 'ctx')
- new_tracker: bfloat16 [16, 2048, 2048], P('dp', None, 'ctx')
The draws below stay inside these ranges and needn't reach their ends.
Inputs may be any that keep to these rules, and one draw needn't show every extreme that they name: `valid_length`: every draw has a replica whose clip fills all 512 positions.
All inputs are finite; a program needn't handle non-finite values.
Results may differ from the reference program's by a relative error of at most 0.0053.
Values may be sent and summed in bfloat16 or wider, within the bound.
A program may use at most 128 MiB of HBM per device.

```python
import jax
import jax.numpy as jnp
from jax import lax

D = 2048
HEADS = 16
HD = 128
KBLK = 128
REPLICAS = 16
SEQ = 512
N_DP = 16


def draw_base(key):
    base = jax.random.fold_in(key, 17)
    query_key, key_key = jax.random.split(base, 2)
    full_shape = (REPLICAS, SEQ, HEADS * HD)
    queries = jax.random.truncated_normal(query_key, -4.0, 4.0, full_shape, jnp.float32)
    key_rows = jax.random.truncated_normal(key_key, -4.0, 4.0, full_shape, jnp.float32)
    return (queries, key_rows)


def draw_queries(key, part):
    queries, key_rows = draw_base(key)
    return queries.astype(jnp.bfloat16)


def draw_key_store(key, part):
    queries, key_rows = draw_base(key)
    return key_rows.astype(jnp.bfloat16)


def draw_valid_length(key, part):
    base = jax.random.fold_in(key, 29)
    length_key, pick_key = jax.random.split(base, 2)
    lengths = jax.random.randint(length_key, (REPLICAS,), SEQ // 8, SEQ + 1)
    longest = jax.random.randint(pick_key, (), 0, REPLICAS)
    return jnp.where(jnp.arange(REPLICAS) == longest, SEQ, lengths).astype(jnp.int32)


def touch_ends(array, own_key, least, largest):
    longest = array.shape.index(max(array.shape))
    spots = []
    for shift in (0, 1):
        where = [jax.random.randint(jax.random.fold_in(own_key, axis), (), 0, length) for axis, length in enumerate(array.shape)]
        where[longest] = (where[longest] + shift) % array.shape[longest]
        spots.append(tuple(where))
    return array.at[spots[0]].set(least).at[spots[1]].set(largest)


def shard_levels(rng, shape, pieces, low, top_value):
    level = 1.0
    for position, blocks in pieces:
        steps = jax.random.uniform(jax.random.fold_in(jax.random.fold_in(rng, 6), position), (blocks,), jnp.float32, low / len(pieces), top_value / len(pieces))
        level = level * jnp.repeat(jnp.exp(steps), shape[position] // blocks).reshape((-1,) + (1,) * (len(shape) - 1 - position))
    return level


def scatter_about(stream_key, extent, width, limit, pieces=(), kind=jnp.bfloat16):
    loudness = shard_levels(stream_key, extent, pieces, -0.22, 0.18) if pieces else 1.0
    array = jax.random.normal(stream_key, extent, jnp.float32) * width * loudness
    return jnp.minimum(jnp.maximum(array, -limit), limit).astype(kind)


def setup_inputs(seed: int = 0) -> dict:
    seeds = jax.random.split(jax.random.key(seed), 11)
    return {
        "queries": draw_queries(jax.random.fold_in(seeds[10], 71), 0),
        "key_store": draw_key_store(jax.random.fold_in(seeds[10], 71), 0),
        "value_store": scatter_about(seeds[2], (REPLICAS, SEQ, HEADS * HD), 1.0, 5.0, ((0, 16), (1, 2))),
        "kv_exponents": touch_ends(jax.random.randint(seeds[3], (REPLICAS, SEQ // KBLK, HEADS), -1, 2), jax.random.fold_in(seeds[3], 1), -1, 1).astype(jnp.int32),
        "valid_length": draw_valid_length(jax.random.fold_in(seeds[10], 71), 0),
        "round_index": jax.random.randint(seeds[5], (1,), 0, 64).astype(jnp.int32),
        "out_grad": scatter_about(seeds[6], (REPLICAS, SEQ, D), 1.0, 6.0, ((0, 16), (2, 2))),
        "params": scatter_about(seeds[7], (REPLICAS, HEADS * HD, D), 1.0, 6.0, ((0, 16), (2, 2))),
        "tracker": scatter_about(seeds[8], (REPLICAS, HEADS * HD, D), 1.0, 6.0, ((0, 16), (2, 2))),
        "old_grad": scatter_about(seeds[9], (REPLICAS, HEADS * HD, D), 1.0, 6.0, ((0, 16), (2, 2))),
    }


step_size = 0.1
masked_score = -1e30


def dequantize(stored, exponents):
    factor = jnp.exp2(exponents.astype(jnp.float32))
    factor = jnp.repeat(jnp.repeat(factor, KBLK, axis=0), HD, axis=1)
    return (stored.astype(jnp.float32) * factor).astype(jnp.bfloat16)


def attend(query_rows, key_rows, value_rows, length):
    positions = jnp.arange(SEQ)
    allowed = (positions[None, :] <= positions[:, None]) & (positions[None, :] < length)
    query_heads = query_rows.astype(jnp.float32).reshape(SEQ, HEADS, HD)
    key_heads = key_rows.astype(jnp.float32).reshape(SEQ, HEADS, HD)
    value_heads = value_rows.astype(jnp.float32).reshape(SEQ, HEADS, HD)
    scores = jnp.einsum("qhd,khd->hqk", query_heads, key_heads) * (HD ** -0.5)
    scores = jnp.where(allowed[None], scores, masked_score)
    row_top = jnp.max(scores, axis=-1, keepdims=True)
    weights = jnp.where(allowed[None], jnp.exp(scores - row_top), 0.0)
    row_total = jnp.sum(weights, axis=-1)
    rounded = lax.optimization_barrier(weights.astype(jnp.bfloat16)).astype(jnp.float32)
    attended = jnp.einsum("hqk,khd->qhd", rounded, value_heads) / jnp.transpose(row_total)[:, :, None]
    return attended.reshape(SEQ, HEADS * HD).astype(jnp.bfloat16)


def reference(queries, key_store, value_store, kv_exponents, valid_length, round_index, out_grad, params, tracker, old_grad):
    levels = N_DP.bit_length() - 1
    bit_now = (round_index[0] % levels).astype(jnp.int32)

    def replica(replica_id):
        partner = jnp.bitwise_xor(replica_id, jnp.left_shift(jnp.int32(1), bit_now)).astype(jnp.int32)
        length = valid_length[replica_id]
        key_rows = dequantize(key_store[replica_id], kv_exponents[replica_id])
        value_rows = dequantize(value_store[replica_id], kv_exponents[replica_id])
        attended = attend(queries[replica_id], key_rows, value_rows, length)
        live_rows = jnp.arange(SEQ)[:, None] < length
        masked = jnp.where(live_rows, out_grad[replica_id], jnp.zeros((), jnp.bfloat16))
        grad_new = jnp.dot(attended.T, masked, preferred_element_type=jnp.float32)
        tracker_sum = 0.5 * (tracker[replica_id].astype(jnp.float32) + tracker[partner].astype(jnp.float32)) + grad_new - old_grad[replica_id].astype(jnp.float32)
        tracker_next = tracker_sum.astype(jnp.bfloat16)
        params_next = (0.5 * (params[replica_id].astype(jnp.float32) + params[partner].astype(jnp.float32)) - step_size * tracker_next.astype(jnp.float32)).astype(jnp.bfloat16)
        return params_next, tracker_next

    new_params, new_tracker = lax.map(replica, jnp.arange(REPLICAS, dtype=jnp.int32))
    return new_params, new_tracker
```

```python
import jax
import jax.numpy as jnp
from jax import lax
from jax.sharding import PartitionSpec as P

HEADS = 16
HD = 128
KBLK = 128


step_size = 0.1
masked_score = -1e30


def from_partner(value, axis, bit):
    mask = 2**bit
    pairs = [(source, source ^ mask) for source in range(lax.axis_size(axis))]
    return lax.ppermute(value, axis, pairs)


def dequantize(stored, exponents):
    factor = jnp.exp2(exponents.astype(jnp.float32))
    factor = jnp.repeat(jnp.repeat(factor, KBLK, axis=0), HD, axis=1)
    return (stored.astype(jnp.float32) * factor).astype(jnp.bfloat16)


def contract_rows(left_rows, right_rows):
    return lax.dot_general(
        left_rows, right_rows, (((0,), (0,)), ((), ())), preferred_element_type=jnp.float32
    )


def gather_ctx(block):
    if lax.axis_size("ctx") != 2:
        return lax.all_gather(block, "ctx", axis=0, tiled=True)
    other = lax.ppermute(block, "ctx", [(0, 1), (1, 0)])
    first = lax.axis_index("ctx") == 0
    return jnp.concatenate(
        (jnp.where(first, block, other), jnp.where(first, other, block)), axis=0
    )


def attention(queries, key_store, value_store, kv_exponents, length):
    tok_rows = queries.shape[1]
    key_rows = dequantize(key_store[0], kv_exponents[0])
    value_rows = dequantize(value_store[0], kv_exponents[0])
    score_scale = HD ** (-0.5)
    query_heads = queries[0].reshape(tok_rows, HEADS, HD)
    query_pos = lax.axis_index("ctx") * tok_rows + jnp.arange(tok_rows)
    key_piece = gather_ctx(key_rows)
    value_piece = gather_ctx(value_rows)
    piece_count = key_piece.shape[0]
    key_pos = jnp.arange(piece_count)
    allowed = (key_pos[None, :] <= query_pos[:, None]) & (key_pos[None, :] < length)
    scores = (
        jnp.einsum(
            "qhd,khd->hqk",
            query_heads,
            key_piece.reshape(piece_count, HEADS, HD),
            preferred_element_type=jnp.float32,
        )
        * score_scale
    )
    scores = jnp.where(allowed[None], scores, masked_score)
    top = jnp.max(scores, axis=-1)
    weights = jnp.where(allowed[None], jnp.exp(scores - top[:, :, None]), 0.0)
    row_total = jnp.sum(weights, axis=-1)
    weighted = jnp.einsum(
        "hqk,khd->hqd",
        weights.astype(jnp.bfloat16),
        value_piece.reshape(piece_count, HEADS, HD),
        preferred_element_type=jnp.float32,
    )
    return (
        jnp.transpose(weighted / row_total[:, :, None], (1, 0, 2))
        .reshape(tok_rows, HEADS * HD)
        .astype(jnp.bfloat16)
    )


def step_with(bit_number):

    def step(
        queries, key_store, value_store, kv_exponents, valid_length,
        out_grad, params, tracker, old_grad,
    ):
        peer_tracker = from_partner(tracker[0], "dp", bit_number)
        peer_params = from_partner(params[0], "dp", bit_number)
        length = valid_length[0]
        seq_rows = out_grad.shape[1]
        live_rows = jnp.arange(seq_rows)[:, None] < length
        masked = jnp.where(live_rows, out_grad[0], jnp.zeros((), jnp.bfloat16))
        attended = attention(queries, key_store, value_store, kv_exponents, length)
        grad_new = contract_rows(gather_ctx(attended), masked)
        grad_own = grad_new - old_grad[0].astype(jnp.float32)
        tracker_sum = (
            0.5 * (tracker[0].astype(jnp.float32) + peer_tracker.astype(jnp.float32)) + grad_own
        )
        new_tracker = tracker_sum.astype(jnp.bfloat16)
        new_params = (
            0.5 * (params[0].astype(jnp.float32) + peer_params.astype(jnp.float32))
            - step_size * new_tracker.astype(jnp.float32)
        ).astype(jnp.bfloat16)
        return (new_params[None], new_tracker[None])

    return step


def shards(
    queries,
    key_store,
    value_store,
    kv_exponents,
    valid_length,
    round_index,
    out_grad,
    params,
    tracker,
    old_grad,
):
    levels = lax.axis_size("dp").bit_length() - 1
    bit_now = round_index[0] % levels
    return lax.switch(
        bit_now,
        [step_with(bit_number) for bit_number in range(levels)],
        queries, key_store, value_store, kv_exponents, valid_length,
        out_grad, params, tracker, old_grad,
    )


def solution(mesh):
    placed = (
        P("dp", "ctx", None),
        P("dp", "ctx", None),
        P("dp", "ctx", None),
        P("dp", "ctx", None),
        P("dp"),
        P(),
        P("dp", None, "ctx"),
        P("dp", None, "ctx"),
        P("dp", None, "ctx"),
        P("dp", None, "ctx"),
    )
    return jax.shard_map(
        shards,
        mesh=mesh,
        in_specs=placed,
        out_specs=(P("dp", None, "ctx"), P("dp", None, "ctx")),
        check_vma=False,
    )
```

```python
import jax
import jax.numpy as jnp
from jax import lax
from jax.experimental import pallas as pl
from jax.experimental.pallas import tpu as pltpu
from jax.sharding import PartitionSpec as P

HEADS = 16
HD = 128
KBLK = 128
QROWS = 256
LAST_ROWS = 256


step_size = 0.1
masked_score = -1e30


def from_partner(value, axis, bit):
    mask = 2**bit
    pairs = [(source, source ^ mask) for source in range(lax.axis_size(axis))]
    return lax.ppermute(value, axis, pairs)


def contract_rows(left_rows, right_rows):
    return lax.dot_general(
        left_rows, right_rows, (((0,), (0,)), ((), ())), preferred_element_type=jnp.float32
    )


def from_other(block):
    return lax.ppermute(block, "ctx", [(0, 1), (1, 0)])


def in_order(own, other, axis):
    first = lax.axis_index("ctx") == 0
    return jnp.concatenate(
        (jnp.where(first, own, other), jnp.where(first, other, own)), axis=axis
    )


def gather_ctx(block, axis):
    if lax.axis_size("ctx") != 2:
        return lax.all_gather(block, "ctx", axis=axis, tiled=True)
    return in_order(block, from_other(block), axis)


def rows_to_heads(block):
    if lax.axis_size("ctx") != 2:
        return lax.all_to_all(block, "ctx", split_axis=1, concat_axis=0, tiled=True)
    half = block.shape[1] // 2
    first = lax.axis_index("ctx") == 0
    kept = jnp.where(first, block[:, :half], block[:, half:])
    sent = jnp.where(first, block[:, half:], block[:, :half])
    return in_order(kept, from_other(sent), 0)


def attend_kernel(meta, scales, q_ref, k_ref, v_ref, out_ref):
    length = meta[0]
    head = meta[1] + pl.program_id(0)
    row0 = pl.program_id(1) * QROWS
    seq = k_ref.shape[0]

    def scaled(ref):
        return jnp.concatenate(
            [
                (
                    ref[pl.ds(block * KBLK, KBLK), :].astype(jnp.float32) * scales[block, head]
                ).astype(jnp.bfloat16)
                for block in range(seq // KBLK)
            ],
            axis=0,
        )

    scores = lax.dot_general(
        q_ref[...], scaled(k_ref), (((1,), (1,)), ((), ())), preferred_element_type=jnp.float32
    ) * (HD ** (-0.5))
    query_pos = row0 + lax.broadcasted_iota(jnp.int32, scores.shape, 0)
    key_pos = lax.broadcasted_iota(jnp.int32, scores.shape, 1)
    allowed = (key_pos <= query_pos) & (key_pos < length)
    scores = jnp.where(allowed, scores, masked_score)
    top = jnp.max(scores, axis=-1, keepdims=True)
    weights = jnp.where(allowed, jnp.exp(scores - top), 0.0)
    total = jnp.sum(weights, axis=-1, keepdims=True)
    weighted = jnp.dot(
        weights.astype(jnp.bfloat16), scaled(v_ref), preferred_element_type=jnp.float32
    )
    out_ref[...] = (weighted / total).astype(jnp.bfloat16)


def attend(queries, keys, values, scales, length):
    seq, width = queries.shape
    heads = width // HD
    meta = jnp.stack((length, lax.axis_index("ctx") * heads)).astype(jnp.int32)
    keys_spec = pl.BlockSpec((seq, HD), lambda h, i: (0, h))
    rows_spec = pl.BlockSpec((QROWS, HD), lambda h, i: (i, h))
    smem = pl.BlockSpec(memory_space=pltpu.SMEM)
    return pl.pallas_call(
        attend_kernel,
        grid=(heads, seq // QROWS),
        in_specs=[smem, smem, rows_spec, keys_spec, keys_spec],
        out_specs=rows_spec,
        out_shape=jax.ShapeDtypeStruct((seq, width), jnp.bfloat16),
        cost_estimate=pl.CostEstimate(
            flops=4 * seq * seq * width,
            bytes_accessed=8 * seq * width,
            transcendentals=seq * seq * heads,
        ),
    )(meta, scales, queries, keys, values)


def average_kernel(own_ref, peer_ref, tracker_ref, *rest):
    out_ref = rest[-1]
    out_ref[...] = (
        0.5 * (own_ref[...].astype(jnp.float32) + peer_ref[...].astype(jnp.float32))
        - step_size * tracker_ref[...].astype(jnp.float32)
    ).astype(jnp.bfloat16)


def average_rows(own, peer_rows, new_tracker, start, filled=None):
    rows, cols = peer_rows.shape
    tile = LAST_ROWS // 2
    here = pl.BlockSpec((tile, cols), lambda i: (i + start // tile, 0))
    operands = [own, peer_rows, new_tracker]
    specs = [here, pl.BlockSpec((tile, cols), lambda i: (i, 0)), here]
    aliases = {}
    if filled is not None:
        operands.append(filled)
        specs.append(pl.BlockSpec(memory_space=pl.ANY))
        aliases = {3: 0}
    return pl.pallas_call(
        average_kernel,
        grid=(rows // tile,),
        in_specs=specs,
        out_specs=here,
        out_shape=jax.ShapeDtypeStruct(own.shape, jnp.bfloat16),
        input_output_aliases=aliases,
        cost_estimate=pl.CostEstimate(
            flops=4 * rows * cols, bytes_accessed=8 * rows * cols, transcendentals=0
        ),
    )(*operands)


def step_with(bit_number):

    def step(
        queries, key_store, value_store, kv_exponents, valid_length,
        out_grad, params, tracker, old_grad,
    ):
        split = params.shape[1] - LAST_ROWS
        peer_tracker = from_partner(tracker[0], "dp", bit_number)
        peer_most = from_partner(params[0, :split], "dp", bit_number)
        peer_last = from_partner(params[0, split:], "dp", bit_number)
        length = valid_length[0]
        seq_rows = out_grad.shape[1]
        live_rows = jnp.arange(seq_rows)[:, None] < length
        masked = jnp.where(live_rows, out_grad[0], jnp.zeros((), jnp.bfloat16))
        scales = gather_ctx(jnp.exp2(kv_exponents[0].astype(jnp.float32)), 0)
        own_heads = attend(
            rows_to_heads(queries[0]),
            rows_to_heads(key_store[0]),
            rows_to_heads(value_store[0]),
            scales,
            length,
        )
        grad_new = contract_rows(gather_ctx(own_heads, 1), masked)
        tracker_sum = (
            0.5 * (tracker[0].astype(jnp.float32) + peer_tracker.astype(jnp.float32))
            + grad_new
            - old_grad[0].astype(jnp.float32)
        )
        new_tracker = tracker_sum.astype(jnp.bfloat16)
        new_params = average_rows(params[0], peer_most, new_tracker, 0)
        new_params = average_rows(params[0], peer_last, new_tracker, split, new_params)
        return (new_params[None], new_tracker[None])

    return step


def shards(
    queries,
    key_store,
    value_store,
    kv_exponents,
    valid_length,
    round_index,
    out_grad,
    params,
    tracker,
    old_grad,
):
    levels = lax.axis_size("dp").bit_length() - 1
    bit_now = round_index[0] % levels
    return lax.switch(
        bit_now,
        [step_with(bit_number) for bit_number in range(levels)],
        queries, key_store, value_store, kv_exponents, valid_length,
        out_grad, params, tracker, old_grad,
    )


def solution(mesh):
    placed = (
        P("dp", "ctx", None),
        P("dp", "ctx", None),
        P("dp", "ctx", None),
        P("dp", "ctx", None),
        P("dp"),
        P(),
        P("dp", None, "ctx"),
        P("dp", None, "ctx"),
        P("dp", None, "ctx"),
        P("dp", None, "ctx"),
    )
    return jax.shard_map(
        shards,
        mesh=mesh,
        in_specs=placed,
        out_specs=(P("dp", None, "ctx"), P("dp", None, "ctx")),
        check_vma=False,
    )
```

```python
import functools

import jax
import jax.numpy as jnp
from jax import lax
from jax.experimental import pallas as pl
from jax.experimental.pallas import tpu as pltpu
from jax.sharding import PartitionSpec as P


HEADS = 16
HD = 128
KBLK = 128
QROWS = 256
LAST_ROWS = 256


step_size = 0.1
masked_score = -1e30


def from_partner(value, axis, bit):
    mask = 2**bit
    pairs = [(source, source ^ mask) for source in range(lax.axis_size(axis))]
    return lax.ppermute(value, axis, pairs)


def contract_rows(left_rows, right_rows):
    return lax.dot_general(
        left_rows, right_rows, (((0,), (0,)), ((), ())), preferred_element_type=jnp.float32
    )


def from_other(block):
    return lax.ppermute(block, "ctx", [(0, 1), (1, 0)])


def in_order(own, other, axis):
    first = lax.axis_index("ctx") == 0
    return jnp.concatenate(
        (jnp.where(first, own, other), jnp.where(first, other, own)), axis=axis
    )


def gather_ctx(block, axis):
    if lax.axis_size("ctx") != 2:
        return lax.all_gather(block, "ctx", axis=axis, tiled=True)
    return in_order(block, from_other(block), axis)


def rows_to_heads(block, group, groups):
    if lax.axis_size("ctx") != 2:
        return lax.all_to_all(block, "ctx", split_axis=1, concat_axis=0, tiled=True)
    width = block.shape[1] // (2 * groups)
    mine = lax.axis_index("ctx")
    kept = lax.dynamic_slice_in_dim(block, (mine * groups + group) * width, width, 1)
    sent = lax.dynamic_slice_in_dim(block, ((1 - mine) * groups + group) * width, width, 1)
    return in_order(kept, from_other(sent), 0)


def attend_kernel(step_heads, meta, scales, q_ref, k_ref, v_ref, out_ref):
    length = meta[0]
    seq = k_ref.shape[0]
    for local in range(step_heads):
        head = meta[1] + pl.program_id(0) * step_heads + local
        cols = pl.ds(local * HD, HD)

        def scaled(ref):
            return jnp.concatenate(
                [
                    (
                        ref[pl.ds(block * KBLK, KBLK), cols].astype(jnp.float32)
                        * scales[block, head]
                    ).astype(jnp.bfloat16)
                    for block in range(seq // KBLK)
                ],
                axis=0,
            )

        keys, values = scaled(k_ref), scaled(v_ref)
        for row0 in range(0, seq, QROWS):
            reach = row0 + QROWS
            scores = lax.dot_general(
                q_ref[pl.ds(row0, QROWS), cols],
                keys[:reach],
                (((1,), (1,)), ((), ())),
                preferred_element_type=jnp.float32,
            ) * (HD ** (-0.5))
            query_pos = row0 + lax.broadcasted_iota(jnp.int32, scores.shape, 0)
            key_pos = lax.broadcasted_iota(jnp.int32, scores.shape, 1)
            allowed = (key_pos <= query_pos) & (key_pos < length)
            scores = jnp.where(allowed, scores, masked_score)
            top = jnp.max(scores, axis=-1, keepdims=True)
            weights = jnp.exp(scores - top)
            total = jnp.sum(weights, axis=-1, keepdims=True)
            weighted = jnp.dot(
                weights.astype(jnp.bfloat16), values[:reach], preferred_element_type=jnp.float32
            )
            out_ref[pl.ds(row0, QROWS), cols] = (weighted / total).astype(jnp.bfloat16)


def attend(queries, keys, values, scales, length, first_head):
    seq, width = queries.shape
    heads = width // HD
    step_heads = 2 if heads % 2 == 0 and seq <= 512 else 1
    meta = jnp.stack((length, first_head)).astype(jnp.int32)
    spec = pl.BlockSpec((seq, step_heads * HD), lambda h: (0, h))
    smem = pl.BlockSpec(memory_space=pltpu.SMEM)
    return pl.pallas_call(
        functools.partial(attend_kernel, step_heads),
        grid=(heads // step_heads,),
        in_specs=[smem, smem, spec, spec, spec],
        out_specs=spec,
        out_shape=jax.ShapeDtypeStruct((seq, width), jnp.bfloat16),
        cost_estimate=pl.CostEstimate(
            flops=4 * seq * seq * width,
            bytes_accessed=8 * seq * width,
            transcendentals=seq * seq * heads,
        ),
    )(meta, scales, queries, keys, values)


def average_kernel(own_ref, peer_ref, tracker_ref, *rest):
    out_ref = rest[-1]
    out_ref[...] = (
        0.5 * (own_ref[...].astype(jnp.float32) + peer_ref[...].astype(jnp.float32))
        - step_size * tracker_ref[...].astype(jnp.float32)
    ).astype(jnp.bfloat16)


def average_rows(own, peer_rows, new_tracker, start, filled=None):
    rows, cols = peer_rows.shape
    tile = LAST_ROWS
    here = pl.BlockSpec((tile, cols), lambda i: (i + start // tile, 0))
    operands = [own, peer_rows, new_tracker]
    specs = [here, pl.BlockSpec((tile, cols), lambda i: (i, 0)), here]
    aliases = {}
    if filled is not None:
        operands.append(filled)
        specs.append(pl.BlockSpec(memory_space=pl.ANY))
        aliases = {3: 0}
    return pl.pallas_call(
        average_kernel,
        grid=(rows // tile,),
        in_specs=specs,
        out_specs=here,
        out_shape=jax.ShapeDtypeStruct(own.shape, jnp.bfloat16),
        input_output_aliases=aliases,
        cost_estimate=pl.CostEstimate(
            flops=4 * rows * cols, bytes_accessed=8 * rows * cols, transcendentals=0
        ),
    )(*operands)


def step_with(bit_number):
    def step(
        queries, key_store, value_store, kv_exponents, valid_length,
        out_grad, params, tracker, old_grad,
    ):
        split = params.shape[1] - LAST_ROWS
        peer_tracker = from_partner(tracker[0], "dp", bit_number)
        peer_most = from_partner(params[0, :split], "dp", bit_number)
        peer_last = from_partner(params[0, split:], "dp", bit_number)
        length = valid_length[0]
        seq_rows = out_grad.shape[1]
        live_rows = jnp.arange(seq_rows)[:, None] < length
        masked = jnp.where(live_rows, out_grad[0], jnp.zeros((), jnp.bfloat16))
        groups = 2 if lax.axis_size("ctx") == 2 else 1
        exponents = gather_ctx(kv_exponents[0], 0)
        pieces = [
            [
                rows_to_heads(block[0], group, groups)
                for block in (key_store, value_store, queries)
            ]
            for group in range(groups)
        ]
        scales = jnp.exp2(exponents.astype(jnp.float32))
        group_heads = HEADS // (lax.axis_size("ctx") * groups)
        parts = []
        for group, (keys, values, rows) in enumerate(pieces):
            first_head = (lax.axis_index("ctx") * groups + group) * group_heads
            own = attend(rows, keys, values, scales, length, first_head)
            parts.append(gather_ctx(own, 1))
        if groups == 1:
            attended = parts[0]
        else:
            width = group_heads * HD
            attended = jnp.concatenate(
                [
                    part[:, side * width : (side + 1) * width]
                    for side in range(2)
                    for part in parts
                ],
                axis=1,
            )
        grad_new = contract_rows(attended, masked)
        tracker_sum = (
            0.5 * (tracker[0].astype(jnp.float32) + peer_tracker.astype(jnp.float32))
            + grad_new
            - old_grad[0].astype(jnp.float32)
        )
        new_tracker = tracker_sum.astype(jnp.bfloat16)
        new_params = average_rows(params[0], peer_most, new_tracker, 0)
        new_params = average_rows(params[0], peer_last, new_tracker, split, new_params)
        return (new_params[None], new_tracker[None])

    return step


def shards(
    queries,
    key_store,
    value_store,
    kv_exponents,
    valid_length,
    round_index,
    out_grad,
    params,
    tracker,
    old_grad,
):
    levels = lax.axis_size("dp").bit_length() - 1
    bit_now = round_index[0] % levels
    return lax.switch(
        bit_now,
        [step_with(bit_number) for bit_number in range(levels)],
        queries, key_store, value_store, kv_exponents, valid_length,
        out_grad, params, tracker, old_grad,
    )


def solution(mesh):
    placed = (
        P("dp", "ctx", None),
        P("dp", "ctx", None),
        P("dp", "ctx", None),
        P("dp", "ctx", None),
        P("dp"),
        P(),
        P("dp", None, "ctx"),
        P("dp", None, "ctx"),
        P("dp", None, "ctx"),
        P("dp", None, "ctx"),
    )
    return jax.shard_map(
        shards,
        mesh=mesh,
        in_specs=placed,
        out_specs=(P("dp", None, "ctx"), P("dp", None, "ctx")),
        check_vma=False,
    )
```

```python
import functools

import jax
import jax.numpy as jnp
from jax import lax
from jax.experimental import pallas as pl
from jax.experimental.pallas import tpu as pltpu
from jax.sharding import PartitionSpec as P


HEADS = 16
HD = 128
KBLK = 128
QROWS = 256
LAST_ROWS = 256
COMBINE_ROWS = 256


step_size = 0.1
masked_score = -1e30


def from_partner(value, axis, bit):
    mask = 2**bit
    pairs = [(source, source ^ mask) for source in range(lax.axis_size(axis))]
    return lax.ppermute(value, axis, pairs)


def contract_rows(left_rows, right_rows):
    return lax.dot_general(
        left_rows, right_rows, (((0,), (0,)), ((), ())), preferred_element_type=jnp.float32
    )


def from_other(block):
    return lax.ppermute(block, "ctx", [(0, 1), (1, 0)])


def in_order(own, other, axis):
    first = lax.axis_index("ctx") == 0
    return jnp.concatenate(
        (jnp.where(first, own, other), jnp.where(first, other, own)), axis=axis
    )


def gather_ctx(block, axis):
    if lax.axis_size("ctx") != 2:
        return lax.all_gather(block, "ctx", axis=axis, tiled=True)
    return in_order(block, from_other(block), axis)


def rows_to_heads(block, group, groups):
    if lax.axis_size("ctx") != 2:
        return lax.all_to_all(block, "ctx", split_axis=1, concat_axis=0, tiled=True)
    width = block.shape[1] // (2 * groups)
    mine = lax.axis_index("ctx")
    kept = lax.dynamic_slice_in_dim(block, (mine * groups + group) * width, width, 1)
    sent = lax.dynamic_slice_in_dim(block, ((1 - mine) * groups + group) * width, width, 1)
    return in_order(kept, from_other(sent), 0)


def attend_kernel(step_heads, meta, scales, q_ref, k_ref, v_ref, out_ref):
    length = meta[0]
    seq = k_ref.shape[0]
    for local in range(step_heads):
        head = meta[1] + pl.program_id(0) * step_heads + local
        cols = pl.ds(local * HD, HD)

        def scaled(ref):
            return jnp.concatenate(
                [
                    (
                        ref[pl.ds(block * KBLK, KBLK), cols].astype(jnp.float32)
                        * scales[block, head]
                    ).astype(jnp.bfloat16)
                    for block in range(seq // KBLK)
                ],
                axis=0,
            )

        keys, values = scaled(k_ref), scaled(v_ref)
        for row0 in range(0, seq, QROWS):
            reach = row0 + QROWS
            scores = lax.dot_general(
                q_ref[pl.ds(row0, QROWS), cols],
                keys[:reach],
                (((1,), (1,)), ((), ())),
                preferred_element_type=jnp.float32,
            ) * (HD ** (-0.5))
            query_pos = row0 + lax.broadcasted_iota(jnp.int32, scores.shape, 0)
            key_pos = lax.broadcasted_iota(jnp.int32, scores.shape, 1)
            allowed = (key_pos <= query_pos) & (key_pos < length)
            scores = jnp.where(allowed, scores, masked_score)
            top = jnp.max(scores, axis=-1, keepdims=True)
            weights = jnp.exp(scores - top)
            total = jnp.sum(weights, axis=-1, keepdims=True)
            weighted = jnp.dot(
                weights.astype(jnp.bfloat16), values[:reach], preferred_element_type=jnp.float32
            )
            out_ref[pl.ds(row0, QROWS), cols] = (weighted / total).astype(jnp.bfloat16)


def attend(queries, keys, values, scales, length, first_head):
    seq, width = queries.shape
    heads = width // HD
    step_heads = 2 if heads % 2 == 0 and seq <= 512 else 1
    meta = jnp.stack((length, first_head)).astype(jnp.int32)
    spec = pl.BlockSpec((seq, step_heads * HD), lambda h: (0, h))
    smem = pl.BlockSpec(memory_space=pltpu.SMEM)
    return pl.pallas_call(
        functools.partial(attend_kernel, step_heads),
        grid=(heads // step_heads,),
        in_specs=[smem, smem, spec, spec, spec],
        out_specs=spec,
        out_shape=jax.ShapeDtypeStruct((seq, width), jnp.bfloat16),
        cost_estimate=pl.CostEstimate(
            flops=4 * seq * seq * width,
            bytes_accessed=8 * seq * width,
            transcendentals=seq * seq * heads,
        ),
    )(meta, scales, queries, keys, values)


def average_kernel(own_ref, peer_ref, tracker_ref, *rest):
    out_ref = rest[-1]
    out_ref[...] = (
        0.5 * (own_ref[...].astype(jnp.float32) + peer_ref[...].astype(jnp.float32))
        - step_size * tracker_ref[...].astype(jnp.float32)
    ).astype(jnp.bfloat16)


def average_rows(own, peer_rows, new_tracker, start, filled=None):
    rows, cols = peer_rows.shape
    tile = LAST_ROWS
    here = pl.BlockSpec((tile, cols), lambda i: (i + start // tile, 0))
    operands = [own, peer_rows, new_tracker]
    peer_spec = pl.BlockSpec((tile, cols), lambda i: (i, 0))
    if rows == tile:
        peer_spec = pl.BlockSpec(memory_space=pltpu.VMEM)
    specs = [here, peer_spec, here]
    aliases = {}
    if filled is not None:
        operands.append(filled)
        specs.append(pl.BlockSpec(memory_space=pl.ANY))
        aliases = {3: 0}
    return pl.pallas_call(
        average_kernel,
        grid=(rows // tile,),
        in_specs=specs,
        out_specs=here,
        out_shape=jax.ShapeDtypeStruct(own.shape, jnp.bfloat16),
        input_output_aliases=aliases,
        cost_estimate=pl.CostEstimate(
            flops=4 * rows * cols, bytes_accessed=8 * rows * cols, transcendentals=0
        ),
    )(*operands)


def combine_kernel(base, att_ref, masked_ref, tracker_ref, peer_tracker_ref, old_ref,
                   params_ref, peer_params_ref, *rest):
    new_tracker_ref, new_params_ref = rest[-2:]
    grad = contract_rows(att_ref[...], masked_ref[...])
    new_tracker = (
        0.5 * (tracker_ref[...].astype(jnp.float32) + peer_tracker_ref[...].astype(jnp.float32))
        + grad
        - old_ref[...].astype(jnp.float32)
    ).astype(jnp.bfloat16)
    new_tracker_ref[...] = new_tracker
    new_params_ref[...] = (
        0.5 * (params_ref[...].astype(jnp.float32) + peer_params_ref[...].astype(jnp.float32))
        - step_size * new_tracker.astype(jnp.float32)
    ).astype(jnp.bfloat16)


def combine_rows(part, row_start, masked, arrays, filled):
    seq, width = part.shape
    cols = masked.shape[1]
    tile = COMBINE_ROWS
    here = pl.BlockSpec((tile, cols), lambda i, base: (base[0] + i, 0))
    specs = [
        pl.BlockSpec((seq, tile), lambda i, base: (0, i)),
        pl.BlockSpec((seq, cols), lambda i, base: (0, 0)),
    ] + [here] * len(arrays)
    aliases = {}
    if filled:
        specs += [pl.BlockSpec(memory_space=pl.ANY)] * 2
        aliases = {3 + len(arrays): 0, 4 + len(arrays): 1}
    shape = jax.ShapeDtypeStruct(arrays[0].shape, jnp.bfloat16)
    return pl.pallas_call(
        combine_kernel,
        grid_spec=pltpu.PrefetchScalarGridSpec(
            num_scalar_prefetch=1,
            grid=(width // tile,),
            in_specs=specs,
            out_specs=[here, here],
        ),
        out_shape=[shape, shape],
        input_output_aliases=aliases,
        cost_estimate=pl.CostEstimate(
            flops=2 * seq * width * cols,
            bytes_accessed=2 * (7 * width * cols + seq * cols + seq * width),
            transcendentals=0,
        ),
    )((row_start // tile).astype(jnp.int32)[None], part, masked, *arrays, *filled)


def step_with(bit_number):
    def step(
        queries, key_store, value_store, kv_exponents, valid_length,
        out_grad, params, tracker, old_grad,
    ):
        by_group = bit_number == 0 and lax.axis_size("ctx") == 2
        split = params.shape[1] - LAST_ROWS
        peer_tracker = from_partner(tracker[0], "dp", bit_number)
        if by_group:
            peer_params = from_partner(params[0], "dp", bit_number)
        else:
            peer_most = from_partner(params[0, :split], "dp", bit_number)
            peer_last = from_partner(params[0, split:], "dp", bit_number)
        length = valid_length[0]
        seq_rows = out_grad.shape[1]
        live_rows = jnp.arange(seq_rows)[:, None] < length
        masked = jnp.where(live_rows, out_grad[0], jnp.zeros((), jnp.bfloat16))
        groups = 2 if lax.axis_size("ctx") == 2 else 1
        exponents = gather_ctx(kv_exponents[0], 0)
        scales = jnp.exp2(exponents.astype(jnp.float32))
        pieces = []
        for group in range(groups):
            pieces.append(
                [
                    rows_to_heads(block[0], group, groups)
                    for block in (key_store, value_store, queries)
                ]
            )
        mine = lax.axis_index("ctx")
        group_heads = HEADS // (lax.axis_size("ctx") * groups)
        width = group_heads * HD
        own_parts = [
            attend(rows, keys, values, scales, length, (mine * groups + group) * group_heads)
            for group, (keys, values, rows) in enumerate(pieces)
        ]
        if by_group:
            arrays = (tracker[0], peer_tracker, old_grad[0], params[0], peer_params)
            done = ()
            other_parts = []
            for own in own_parts:
                other_parts.append(from_other(own))
            for side, parts in ((mine, own_parts), (1 - mine, other_parts)):
                for group, part in enumerate(parts):
                    row_start = (side * groups + group) * width
                    done = combine_rows(part, row_start, masked, arrays, done)
            return (done[1][None], done[0][None])
        parts = [gather_ctx(own, 1) for own in own_parts]
        if groups == 1:
            attended = parts[0]
        else:
            attended = jnp.concatenate(
                [
                    part[:, side * width : (side + 1) * width]
                    for side in range(2)
                    for part in parts
                ],
                axis=1,
            )
        grad_new = contract_rows(attended, masked)
        tracker_sum = (
            0.5 * (tracker[0].astype(jnp.float32) + peer_tracker.astype(jnp.float32))
            + grad_new
            - old_grad[0].astype(jnp.float32)
        )
        new_tracker = tracker_sum.astype(jnp.bfloat16)
        new_params = average_rows(params[0], peer_most, new_tracker, 0)
        new_params = average_rows(params[0], peer_last, new_tracker, split, new_params)
        return (new_params[None], new_tracker[None])

    return step


def shards(
    queries,
    key_store,
    value_store,
    kv_exponents,
    valid_length,
    round_index,
    out_grad,
    params,
    tracker,
    old_grad,
):
    levels = lax.axis_size("dp").bit_length() - 1
    bit_now = round_index[0] % levels
    return lax.switch(
        bit_now,
        [step_with(bit_number) for bit_number in range(levels)],
        queries, key_store, value_store, kv_exponents, valid_length,
        out_grad, params, tracker, old_grad,
    )


def solution(mesh):
    placed = (
        P("dp", "ctx", None),
        P("dp", "ctx", None),
        P("dp", "ctx", None),
        P("dp", "ctx", None),
        P("dp"),
        P(),
        P("dp", None, "ctx"),
        P("dp", None, "ctx"),
        P("dp", None, "ctx"),
        P("dp", None, "ctx"),
    )
    return jax.shard_map(
        shards,
        mesh=mesh,
        in_specs=placed,
        out_specs=(P("dp", None, "ctx"), P("dp", None, "ctx")),
        check_vma=False,
    )
```

```python
import functools

import jax
import jax.numpy as jnp
from jax import lax
from jax.experimental import pallas as pl
from jax.experimental.pallas import tpu as pltpu
from jax.sharding import PartitionSpec as P


HEADS = 16
HD = 128
KBLK = 128
QROWS = 256
LAST_ROWS = 256
COMBINE_ROWS = 256


step_size = 0.1
masked_score = -1e30


def from_partner(value, axis, bit):
    mask = 2**bit
    pairs = [(source, source ^ mask) for source in range(lax.axis_size(axis))]
    return lax.ppermute(value, axis, pairs)


def contract_rows(left_rows, right_rows):
    return lax.dot_general(
        left_rows, right_rows, (((0,), (0,)), ((), ())), preferred_element_type=jnp.float32
    )


def from_other(block):
    return lax.ppermute(block, "ctx", [(0, 1), (1, 0)])


def in_order(own, other, axis):
    first = lax.axis_index("ctx") == 0
    return jnp.concatenate(
        (jnp.where(first, own, other), jnp.where(first, other, own)), axis=axis
    )


def gather_ctx(block, axis):
    if lax.axis_size("ctx") != 2:
        return lax.all_gather(block, "ctx", axis=axis, tiled=True)
    return in_order(block, from_other(block), axis)


def rows_to_heads(block, group, groups):
    if lax.axis_size("ctx") != 2:
        return (lax.all_to_all(block, "ctx", split_axis=1, concat_axis=0, tiled=True),)
    width = block.shape[1] // (2 * groups)
    mine = lax.axis_index("ctx")
    kept = lax.dynamic_slice_in_dim(block, (mine * groups + group) * width, width, 1)
    sent = lax.dynamic_slice_in_dim(block, ((1 - mine) * groups + group) * width, width, 1)
    return kept, from_other(sent)


def attend_kernel(step_heads, meta, scales, q_ref, k_ref, v_ref, out_ref):
    length = meta[0]
    seq = k_ref.shape[0]
    for local in range(step_heads):
        head = meta[1] + pl.program_id(0) * step_heads + local
        cols = pl.ds(local * HD, HD)

        def scaled(ref):
            return jnp.concatenate(
                [
                    (
                        ref[pl.ds(block * KBLK, KBLK), cols].astype(jnp.float32)
                        * scales[block, head]
                    ).astype(jnp.bfloat16)
                    for block in range(seq // KBLK)
                ],
                axis=0,
            )

        keys, values = scaled(k_ref), scaled(v_ref)
        for row0 in range(0, seq, QROWS):
            reach = row0 + QROWS
            scores = lax.dot_general(
                q_ref[pl.ds(row0, QROWS), cols],
                keys[:reach],
                (((1,), (1,)), ((), ())),
                preferred_element_type=jnp.float32,
            ) * (HD ** (-0.5))
            query_pos = row0 + lax.broadcasted_iota(jnp.int32, scores.shape, 0)
            key_pos = lax.broadcasted_iota(jnp.int32, scores.shape, 1)
            allowed = (key_pos <= query_pos) & (key_pos < length)
            scores = jnp.where(allowed, scores, masked_score)
            top = jnp.max(scores, axis=-1, keepdims=True)
            weights = jnp.exp(scores - top)
            total = jnp.sum(weights, axis=-1, keepdims=True)
            weighted = jnp.dot(
                weights.astype(jnp.bfloat16), values[:reach], preferred_element_type=jnp.float32
            )
            out_ref[pl.ds(row0, QROWS), cols] = (weighted / total).astype(jnp.bfloat16)


def attend(queries, keys, values, scales, length, first_head):
    seq, width = queries.shape
    heads = width // HD
    step_heads = 2 if heads % 2 == 0 and seq <= 512 else 1
    meta = jnp.stack((length, first_head)).astype(jnp.int32)
    spec = pl.BlockSpec((seq, step_heads * HD), lambda h: (0, h))
    smem = pl.BlockSpec(memory_space=pltpu.SMEM)
    return pl.pallas_call(
        functools.partial(attend_kernel, step_heads),
        grid=(heads // step_heads,),
        in_specs=[smem, smem, spec, spec, spec],
        out_specs=spec,
        out_shape=jax.ShapeDtypeStruct((seq, width), jnp.bfloat16),
        cost_estimate=pl.CostEstimate(
            flops=4 * seq * seq * width,
            bytes_accessed=8 * seq * width,
            transcendentals=seq * seq * heads,
        ),
    )(meta, scales, queries, keys, values)


def average_kernel(own_ref, peer_ref, tracker_ref, *rest):
    out_ref = rest[-1]
    out_ref[...] = (
        0.5 * (own_ref[...].astype(jnp.float32) + peer_ref[...].astype(jnp.float32))
        - step_size * tracker_ref[...].astype(jnp.float32)
    ).astype(jnp.bfloat16)


def average_rows(own, peer_rows, new_tracker, start, filled=None):
    rows, cols = peer_rows.shape
    tile = LAST_ROWS
    here = pl.BlockSpec((tile, cols), lambda i: (i + start // tile, 0))
    operands = [own, peer_rows, new_tracker]
    peer_spec = pl.BlockSpec((tile, cols), lambda i: (i, 0))
    if rows == tile:
        peer_spec = pl.BlockSpec(memory_space=pltpu.VMEM)
    specs = [here, peer_spec, here]
    aliases = {}
    if filled is not None:
        operands.append(filled)
        specs.append(pl.BlockSpec(memory_space=pl.ANY))
        aliases = {3: 0}
    return pl.pallas_call(
        average_kernel,
        grid=(rows // tile,),
        in_specs=specs,
        out_specs=here,
        out_shape=jax.ShapeDtypeStruct(own.shape, jnp.bfloat16),
        input_output_aliases=aliases,
        cost_estimate=pl.CostEstimate(
            flops=4 * rows * cols, bytes_accessed=8 * rows * cols, transcendentals=0
        ),
    )(*operands)


def combine_kernel(base, att_ref, masked_ref, tracker_ref, peer_tracker_ref, old_ref,
                   params_ref, peer_params_ref, *rest):
    new_tracker_ref, new_params_ref = rest[-2:]
    grad = contract_rows(att_ref[...], masked_ref[...])
    new_tracker = (
        0.5 * (tracker_ref[...].astype(jnp.float32) + peer_tracker_ref[...].astype(jnp.float32))
        + grad
        - old_ref[...].astype(jnp.float32)
    ).astype(jnp.bfloat16)
    new_tracker_ref[...] = new_tracker
    new_params_ref[...] = (
        0.5 * (params_ref[...].astype(jnp.float32) + peer_params_ref[...].astype(jnp.float32))
        - step_size * new_tracker.astype(jnp.float32)
    ).astype(jnp.bfloat16)


def combine_rows(part, row_start, masked, arrays, filled):
    seq, width = part.shape
    cols = masked.shape[1]
    tile = COMBINE_ROWS
    here = pl.BlockSpec((tile, cols), lambda i, base: (base[0] + i, 0))
    specs = [
        pl.BlockSpec((seq, tile), lambda i, base: (0, i)),
        pl.BlockSpec((seq, cols), lambda i, base: (0, 0)),
    ] + [here] * len(arrays)
    aliases = {}
    if filled:
        specs += [pl.BlockSpec(memory_space=pl.ANY)] * 2
        aliases = {3 + len(arrays): 0, 4 + len(arrays): 1}
    shape = jax.ShapeDtypeStruct(arrays[0].shape, jnp.bfloat16)
    return pl.pallas_call(
        combine_kernel,
        grid_spec=pltpu.PrefetchScalarGridSpec(
            num_scalar_prefetch=1,
            grid=(width // tile,),
            in_specs=specs,
            out_specs=[here, here],
        ),
        out_shape=[shape, shape],
        input_output_aliases=aliases,
        cost_estimate=pl.CostEstimate(
            flops=2 * seq * width * cols,
            bytes_accessed=2 * (7 * width * cols + seq * cols + seq * width),
            transcendentals=0,
        ),
    )((row_start // tile).astype(jnp.int32)[None], part, masked, *arrays, *filled)


def step_with(bit_number):
    def step(
        queries, key_store, value_store, kv_exponents, valid_length,
        out_grad, params, tracker, old_grad,
    ):
        by_group = bit_number == 0 and lax.axis_size("ctx") == 2
        split = params.shape[1] - LAST_ROWS
        peer_tracker = from_partner(tracker[0], "dp", bit_number)
        if by_group:
            peer_params = from_partner(params[0], "dp", bit_number)
        else:
            peer_most = from_partner(params[0, :split], "dp", bit_number)
            peer_last = from_partner(params[0, split:], "dp", bit_number)
        length = valid_length[0]
        seq_rows = out_grad.shape[1]
        live_rows = jnp.arange(seq_rows)[:, None] < length
        masked = jnp.where(live_rows, out_grad[0], jnp.zeros((), jnp.bfloat16))
        groups = 2 if lax.axis_size("ctx") == 2 else 1
        exponents = gather_ctx(kv_exponents[0], 0)
        scales = jnp.exp2(exponents.astype(jnp.float32))
        pieces = []
        for group in range(groups):
            pieces.append(
                [
                    rows_to_heads(block[0], group, groups)
                    for block in (key_store, value_store, queries)
                ]
            )
        mine = lax.axis_index("ctx")
        group_heads = HEADS // (lax.axis_size("ctx") * groups)
        width = group_heads * HD
        own_parts = []
        for group, piece in enumerate(pieces):
            if own_parts:
                piece, _ = lax.optimization_barrier((piece, own_parts[-1]))
            keys, values, rows = (
                in_order(*halves, 0) if len(halves) == 2 else halves[0] for halves in piece
            )
            first_head = (mine * groups + group) * group_heads
            own_parts.append(attend(rows, keys, values, scales, length, first_head))
        if by_group:
            arrays = (tracker[0], peer_tracker, old_grad[0], params[0], peer_params)
            done = ()
            other_parts = []
            for own in own_parts:
                other_parts.append(from_other(own))
            for side, parts in ((mine, own_parts), (1 - mine, other_parts)):
                for group, part in enumerate(parts):
                    row_start = (side * groups + group) * width
                    done = combine_rows(part, row_start, masked, arrays, done)
            return (done[1][None], done[0][None])
        parts = [gather_ctx(own, 1) for own in own_parts]
        if groups == 1:
            attended = parts[0]
        else:
            attended = jnp.concatenate(
                [
                    part[:, side * width : (side + 1) * width]
                    for side in range(2)
                    for part in parts
                ],
                axis=1,
            )
        grad_new = contract_rows(attended, masked)
        tracker_sum = (
            0.5 * (tracker[0].astype(jnp.float32) + peer_tracker.astype(jnp.float32))
            + grad_new
            - old_grad[0].astype(jnp.float32)
        )
        new_tracker = tracker_sum.astype(jnp.bfloat16)
        new_params = average_rows(params[0], peer_most, new_tracker, 0)
        new_params = average_rows(params[0], peer_last, new_tracker, split, new_params)
        return (new_params[None], new_tracker[None])

    return step


def shards(
    queries,
    key_store,
    value_store,
    kv_exponents,
    valid_length,
    round_index,
    out_grad,
    params,
    tracker,
    old_grad,
):
    levels = lax.axis_size("dp").bit_length() - 1
    bit_now = round_index[0] % levels
    return lax.switch(
        bit_now,
        [step_with(bit_number) for bit_number in range(levels)],
        queries, key_store, value_store, kv_exponents, valid_length,
        out_grad, params, tracker, old_grad,
    )


def solution(mesh):
    placed = (
        P("dp", "ctx", None),
        P("dp", "ctx", None),
        P("dp", "ctx", None),
        P("dp", "ctx", None),
        P("dp"),
        P(),
        P("dp", None, "ctx"),
        P("dp", None, "ctx"),
        P("dp", None, "ctx"),
        P("dp", None, "ctx"),
    )
    return jax.shard_map(
        shards,
        mesh=mesh,
        in_specs=placed,
        out_specs=(P("dp", None, "ctx"), P("dp", None, "ctx")),
        check_vma=False,
    )
```
